128 devices in a mesh: dp: 4 (over y), dict: 32 (over x, z, core).
Axes of the slice: x: 4, y: 4, z: 4, core: 2. Of those that a mesh axis runs over, the one named last changes fastest.
Arguments:
- acts: bfloat16 [8192, 8192], P('dict', 'dp'), may hold values from -6 to 6
- lists: int32 [512, 2], P('dict'), may hold values from 0 to 31, all different within a row; in each aligned block of 16 rows (0 to 15, 16 to 31, ...) at most 2 rows name the same one
- w_enc: bfloat16 [8192, 32768], P('dp', 'dict'), may hold values from -0.0625 to 0.0625
- w_dec: bfloat16 [32768, 8192], P('dict', 'dp'), may hold values from -0.1875 to 0.1875
- b_enc: bfloat16 [32768], P('dict'), may hold values from -3 to 3
- b_dec: bfloat16 [8192], P('dp'), may hold values from -3 to 3
Outputs:
- grad_enc: bfloat16 [8192, 32768], P('dp', 'dict')
- grad_dec: bfloat16 [32768, 8192], P('dict', 'dp')
The draws below stay inside these ranges and needn't reach their ends.
Inputs may be any that keep to these rules, and one draw needn't show every extreme that they name: Each row block lists 2 different panels. Among the 16 row blocks of one index of dict, no panel is listed by more than 2 blocks, and some panel is listed by exactly 2.
All inputs are finite; a program needn't handle non-finite values.
Results may differ from the reference program's by a relative error of at most 0.0057.
Values may be sent and summed in bfloat16 or wider, within the bound.
No kernel may reach another device: no remote copies, remote signals or barrier semaphores. Data moves between devices by JAX's collectives and lax.ppermute only.
A program may use at most 128 MiB of HBM per device.

```python
import math
import jax
import jax.numpy as jnp
import numpy as np
from jax import lax

D = 8192
PANEL = 1024
ROWB = 16
BLK_DEV = 16
ACTIVE = 2
PANELS = 32
LATENTS = 32768
CAP = 2
BLOCKS = 512
ROWS = 8192
N_DICT = 32


def block_scale(rng, shape, cuts, least, largest):
    loudness = 1.0
    for position, shards_of in cuts:
        draws = jax.random.uniform(jax.random.fold_in(jax.random.fold_in(rng, 6), position), (shards_of,), jnp.float32, least / len(cuts), largest / len(cuts))
        loudness = loudness * jnp.repeat(jnp.exp(draws), shape[position] // shards_of).reshape((-1,) + (1,) * (len(shape) - 1 - position))
    return loudness


def routed_block(rng, own, number, rows, number_of, top, reach, slope):
    sequence = jax.random.permutation(rng, number_of)
    heavy_load, common = portions_of(number_of, rows * top, reach, slope, True), portions_of(number_of, rows * top, reach, slope, False)
    places = jnp.arange(number_of)

    def named(sizes, rotation):
        used = int((sizes > 0).sum())
        fixed = max(1, used // 4)
        shifted = fixed + (places - fixed + rotation * (used - fixed)) % max(1, number_of - fixed)
        return jnp.zeros((number_of,), jnp.int32).at[sequence[jnp.where(places < fixed, places, shifted)]].set(jnp.asarray(sizes, jnp.int32))

    sizes = jnp.where(number % 4 == 0, named(heavy_load, number // 4), named(common, number - number // 4 - 1))
    mixed = jax.random.permutation(jax.random.fold_in(own, 3), number_of)
    source_of, sink = mixed[0:number_of // 2 * 2:2], mixed[1:number_of // 2 * 2:2]
    margin = jnp.minimum(sizes[source_of] - 1, reach - sizes[sink]) // 2
    margin = jnp.where((source_of == sequence[0]) | (sink == sequence[0]) | (sizes[sink] == 0), 0, jnp.maximum(margin, 0))
    shifted = jax.random.randint(jax.random.fold_in(own, 4), (number_of // 2,), 0, 1 << 20) % (margin + 1)
    sizes = sizes.at[source_of].add(-shifted).at[sink].add(shifted)
    items = jnp.searchsorted(jnp.cumsum(sizes), jnp.arange(rows * top), side="right").astype(jnp.int32)
    grid = items.reshape(top, rows).T
    grid = grid[jax.random.permutation(jax.random.fold_in(own, 1), rows)]
    rotation = jax.random.randint(jax.random.fold_in(own, 2), (rows, 1), 0, top)
    return jnp.take_along_axis(grid, (jnp.arange(top)[None, :] + rotation) % top, axis=1)


def portions_of(count, total, most, lean, full):
    portions = [(1 << 20) // math.isqrt(grade ** lean) + 1 for grade in range(1, count + 1)]
    largest = most if full else min(most, max(-(-total // count), total * portions[0] // sum(portions)))
    least = 1 if total - largest >= count - 1 else 0
    counts, spare = [largest] + [least] * (count - 1), total - largest - least * (count - 1)
    while spare > 0:
        movable = [i for i in range(1, count) if counts[i] < largest] or [i for i in range(1, count) if counts[i] < most]
        mass, remaining = sum([portions[i] for i in movable]), spare
        for i in movable:
            addition = min(most - counts[i], max(1, remaining * portions[i] // mass), spare)
            counts[i] = counts[i] + addition
            spare = spare - addition
    return np.array(counts)


def normal_values(own_key, shape, width, reach, shards=(), held_as=jnp.bfloat16):
    gain = block_scale(own_key, shape, shards, -0.22, 0.18) if shards else 1.0
    result = jax.random.normal(own_key, shape, jnp.float32) * width * gain
    return jnp.minimum(jnp.maximum(result, -reach), reach).astype(held_as)


def setup_inputs(seed: int = 0) -> dict:
    keys = jax.random.split(jax.random.key(seed), 7)
    acts = normal_values(keys[0], (ROWS, D), 1.0, 6.0, ((0, 32), (1, 4)))
    lists_keys = jax.random.split(jax.random.fold_in(keys[1], 1), BLOCKS // BLK_DEV)
    lists_turns = jax.random.permutation(jax.random.fold_in(keys[1], 3), BLOCKS // BLK_DEV)
    lists = jax.vmap(lambda own, number: routed_block(jax.random.fold_in(keys[1], 2), own, number, BLK_DEV, PANELS, ACTIVE, CAP, 2))(lists_keys, lists_turns).reshape((BLOCKS, ACTIVE))
    w_enc = normal_values(keys[2], (D, LATENTS), D ** -0.5, 0.0625, ((0, 4), (1, 32)))
    w_dec = normal_values(keys[3], (LATENTS, D), PANEL ** -0.5, 0.1875, ((0, 32), (1, 4)))
    b_enc = normal_values(keys[4], (LATENTS,), 0.5, 3.0, ((0, 32),))
    b_dec = normal_values(keys[5], (D,), 0.5, 3.0, ((0, 4),))
    return {"acts": acts, "lists": lists, "w_enc": w_enc, "w_dec": w_dec, "b_enc": b_enc, "b_dec": b_dec}


def reference(acts, lists, w_enc, w_dec, b_enc, b_dec):
    blocks_x = acts.reshape(BLOCKS, ROWB, D)
    most_blocks = N_DICT * CAP

    def members(panel_id):
        listed = jnp.any(lists == panel_id, axis=1)
        member_idx = jnp.nonzero(listed, size=most_blocks, fill_value=BLOCKS)[0].astype(jnp.int32)
        valid = member_idx < BLOCKS
        safe_idx = jnp.minimum(member_idx, BLOCKS - 1).astype(jnp.int32)
        return member_idx, safe_idx, valid

    def panel_weights(panel_id):
        start = (panel_id * PANEL).astype(jnp.int32)
        enc_panel = lax.dynamic_slice_in_dim(w_enc, start, PANEL, 1)
        dec_panel = lax.dynamic_slice_in_dim(w_dec, start, PANEL, 0)
        bias_panel = lax.dynamic_slice_in_dim(b_enc, start, PANEL, 0)
        return enc_panel, dec_panel, bias_panel

    def forward(rebuilt, panel_id):
        member_idx, safe_idx, valid = members(panel_id)
        enc_panel, dec_panel, bias_panel = panel_weights(panel_id)
        rows_sel = jnp.where(valid[:, None, None], blocks_x[safe_idx], jnp.zeros((), blocks_x.dtype))
        preact = jnp.dot(rows_sel.reshape(-1, D), enc_panel, preferred_element_type=jnp.float32) + bias_panel.astype(jnp.float32)
        activity = (jnp.maximum(preact, 0.0) ** 2).astype(jnp.bfloat16)
        part = jnp.dot(activity, dec_panel, preferred_element_type=jnp.float32).astype(jnp.bfloat16)
        rebuilt = rebuilt.at[member_idx].add(part.reshape(most_blocks, ROWB, D).astype(jnp.float32), mode="drop")
        return rebuilt, (preact, activity)

    start_sum = jnp.zeros((BLOCKS, ROWB, D), jnp.float32)
    panel_ids = jnp.arange(PANELS, dtype=jnp.int32)
    rebuilt, (preacts, activities) = lax.scan(forward, start_sum, panel_ids)
    rebuilt = rebuilt + b_dec.astype(jnp.float32)
    residual_g = ((rebuilt - blocks_x.astype(jnp.float32)) * (1.0 / ROWB)).astype(jnp.bfloat16)

    def backward(inputs):
        panel_id, preact, activity = inputs
        member_idx, safe_idx, valid = members(panel_id)
        enc_panel, dec_panel, bias_panel = panel_weights(panel_id)
        rows_sel = jnp.where(valid[:, None, None], blocks_x[safe_idx], jnp.zeros((), blocks_x.dtype)).reshape(-1, D)
        resid_sel = jnp.where(valid[:, None, None], residual_g[safe_idx], jnp.zeros((), residual_g.dtype)).reshape(-1, D)
        dec_grad = jnp.dot(activity.T, resid_sel, preferred_element_type=jnp.float32).astype(jnp.bfloat16)
        dact = jnp.dot(resid_sel, dec_panel.T, preferred_element_type=jnp.float32)
        grad_pre = (dact * 2.0 * jnp.maximum(preact, 0.0)).astype(jnp.bfloat16)
        enc_grad = jnp.dot(rows_sel.T, grad_pre, preferred_element_type=jnp.float32).astype(jnp.bfloat16)
        return enc_grad, dec_grad

    enc_stack, dec_stack = lax.map(backward, (panel_ids, preacts, activities))
    grad_enc = jnp.transpose(enc_stack, (1, 0, 2)).reshape(D, LATENTS)
    grad_dec = dec_stack.reshape(LATENTS, D)
    return grad_enc, grad_dec
```

```python
import jax
import jax.numpy as jnp
from jax import lax
from jax.experimental import pallas as pl
from jax.experimental.pallas import tpu as pltpu
from jax.sharding import PartitionSpec as P


CHUNKS = 2
F32 = jnp.float32
BF16 = jnp.bfloat16
VMEM = pltpu.VMEM


def dot(a, b, dims=((1,), (0,))):
    return lax.dot_general(a, b, (dims, ((), ())), preferred_element_type=F32)


def after(value, *others):
    return lax.optimization_barrier((value,) + others)[0]


def ring(size, shift):
    return [(i, (i + shift) % size) for i in range(size)]


def params(mib=12):
    return pltpu.CompilerParams(vmem_limit_bytes=mib * 1024 * 1024)


def near(value):
    return pltpu.with_memory_space_constraint(value, VMEM)


def far(value):
    return pltpu.with_memory_space_constraint(value, pltpu.HBM)


def whole():
    return pl.BlockSpec(memory_space=VMEM)


def split_matmul(me, rows4, lane, half, weight, transposed, size):
    peers, _, slot_rows, inner = rows4.shape
    halves = 2 if half is None else 1
    my_peers = peers * halves // 2
    first = 0 if half is None else half * my_peers
    count = my_peers * slot_rows
    quarter = count // (size * halves)
    outer = weight.shape[0] if transposed else weight.shape[1]
    tile = min(256, outer)

    def body(me_ref, x_any, w_any, own_ref, *rest):
        sends, (acc, x_ref, w_ref, x_sem, w_sem) = rest[:-5], rest[-5:]
        x_copy = pltpu.make_async_copy(x_any.at[pl.ds(first, my_peers), lane], x_ref, x_sem)
        x_copy.start()

        def fetch(n):
            cols = pl.ds(pl.multiple_of(n * tile, tile), tile)
            source = w_any.at[cols, :] if transposed else w_any.at[:, cols]
            return pltpu.make_async_copy(source, w_ref.at[n], w_sem.at[n])

        for n in range(outer // tile):
            fetch(n).start()
        x_copy.wait()

        @pl.loop(0, outer // tile)
        def _(n):
            fetch(n).wait()
            rows = x_ref[...].reshape(count, inner)
            dims = ((1,), (1,)) if transposed else ((1,), (0,))
            acc[:, pl.ds(pl.multiple_of(n * tile, tile), tile)] = dot(rows, w_ref[n], dims)

        mine = me_ref[0]

        for h in range(halves):
            to = pl.ds(h * quarter, quarter)

            def piece(index):
                start = pl.multiple_of((index + h * size) * quarter, quarter)
                return acc[pl.ds(start, quarter), :]

            own_ref[to, :] = piece(mine)
            for shift in range(1, size):
                sends[shift - 1][to, :] = piece(lax.rem(mine + shift, size)).astype(BF16)

    return pl.pallas_call(
        body,
        in_specs=[pl.BlockSpec(memory_space=pltpu.SMEM)] + [pl.BlockSpec(memory_space=pl.ANY), pl.BlockSpec(memory_space=pltpu.HBM)],
        out_specs=[whole()] * size,
        out_shape=[jax.ShapeDtypeStruct((halves * quarter, outer), F32)]
        + [jax.ShapeDtypeStruct((halves * quarter, outer), BF16)] * (size - 1),
        scratch_shapes=[
            pltpu.VMEM((count, outer), F32),
            pltpu.VMEM((my_peers, slot_rows, inner), BF16),
            pltpu.VMEM((outer // tile, tile, inner) if transposed else (outer // tile, inner, tile), BF16),
            pltpu.SemaphoreType.DMA,
            pltpu.SemaphoreType.DMA((outer // tile,)),
        ],
        compiler_params=params(20),
        name="split_matmul",
    )(me, rows4, weight)


def assemble(me, parts, out_ref, size):
    quarter = out_ref.shape[0] // (2 * size)
    for i, part in enumerate(parts):
        owner = lax.rem(me + size - i % size, size)
        for j in range(part.shape[0] // quarter):
            index = owner + (i // size + j) * size
            to = pl.ds(pl.multiple_of(index * quarter, quarter), quarter)
            out_ref[to, :] = part[pl.ds(j * quarter, quarter), :]


def decode(me, pieces, w_dec, peers, slot_rows, lanes, lane, size):
    count = peers * slot_rows
    inner, outer = w_dec.shape
    tile = 512

    def body(me_ref, *refs):
        parts, w_ref, out_ref, act_ref = refs[:-3], refs[-3], refs[-2], refs[-1]
        step = pl.program_id(0)

        @pl.when(step == 0)
        def _():
            assemble(me_ref[0], parts, act_ref, size)

        part = dot(act_ref[...], w_ref[...]).astype(BF16)
        out_ref[...] = part.reshape(peers, 1, slot_rows, tile)

    return pl.pallas_call(
        body,
        grid=(outer // tile,),
        in_specs=[pl.BlockSpec(memory_space=pltpu.SMEM)]
        + [whole()] * len(pieces)
        + [pl.BlockSpec((inner, tile), lambda n: (0, n))],
        out_specs=[
            pl.BlockSpec((peers, 1, slot_rows, tile), lambda n: (0, lane, 0, n)),
            pl.BlockSpec((count, inner), lambda n: (0, 0)),
        ],
        out_shape=[
            pltpu.HBM((peers, lanes, slot_rows, outer), BF16),
            pltpu.HBM((count, inner), BF16),
        ],
        compiler_params=params(),
        name="decode",
    )(me, *pieces, w_dec)


def residual_rows(selector, returned, lane, x, bias_dec, scale, target, target_lane):
    peers, _, slot_rows, cols = returned.shape
    count = peers * slot_rows
    home = selector.shape[1]
    tile = 512

    def body(sel_ref, got_ref, x_ref, b_ref, *rest):
        out_ref = rest[-1]
        sel = sel_ref[...]
        rebuilt = dot(sel, got_ref[...].reshape(count, tile), ((0,), (0,))) + b_ref[...]
        residual = ((rebuilt - x_ref[...].astype(F32)) * scale).astype(BF16)
        out_ref[...] = dot(sel, residual).astype(BF16).reshape(peers, 1, slot_rows, tile)

    in_specs = [
        whole(),
        pl.BlockSpec((peers, 1, slot_rows, tile), lambda n: (0, lane, 0, n)),
        pl.BlockSpec((home, tile), lambda n: (0, n)),
        pl.BlockSpec((1, tile), lambda n: (0, n)),
    ]
    operands = [selector, returned, x, bias_dec]
    aliases = {}
    lanes = 1
    if target is not None:
        in_specs.append(pl.BlockSpec(memory_space=pltpu.HBM))
        operands.append(target)
        aliases = {4: 0}
        lanes = target.shape[1]
    return pl.pallas_call(
        body,
        grid=(cols // tile,),
        in_specs=in_specs,
        out_specs=pl.BlockSpec((peers, 1, slot_rows, tile), lambda n: (0, target_lane, 0, n)),
        out_shape=pltpu.HBM((peers, lanes, slot_rows, cols), BF16),
        input_output_aliases=aliases,
        compiler_params=params(),
        name="residual_rows",
    )(*operands)


def outer_sum(me, left, left_lane, right, right_lane, base, size, inside):
    pieces = right_lane is None
    if left_lane is None:
        count, wide = left.shape
    else:
        count, wide = left.shape[0] * left.shape[2], left.shape[3]
    out_cols = right[0].shape[-1]
    tile = 512
    last = base is not None

    def body(me_ref, left_ref, *refs):
        right_refs = refs[: len(right)]
        out_ref = refs[len(right) + (1 if last else 0)]
        step = pl.program_id(0)
        here = pl.ds(pl.multiple_of(step * tile, tile), tile)
        lhs = left_ref[...].reshape(count, wide)
        if pieces:
            rows_ref = refs[-1]

            @pl.when(step == 0)
            def _():
                assemble(me_ref[0], right_refs, rows_ref, size)

            rhs = rows_ref[:, here]
        else:
            rhs = right_refs[0][...].reshape(count, tile)
        total = dot(lhs, rhs, ((0,), (0,)))
        if last:
            base_ref = refs[len(right)]
            more = base_ref[:, here] if inside else base_ref[...]
            out_ref[...] = (total + more).astype(BF16)
        elif inside:
            out_ref[:, here] = total
        else:
            out_ref[...] = total

    column_block = pl.BlockSpec((wide, tile), lambda n: (0, n))
    in_specs = [pl.BlockSpec(memory_space=pltpu.SMEM)]
    operands = [me, left]
    if left_lane is None:
        in_specs.append(pl.BlockSpec((count, wide), lambda n: (0, 0)))
    else:
        operands[1] = near(left)
        in_specs.append(whole())
    if pieces:
        in_specs += [whole()] * len(right)
    else:
        peers, _, slot_rows, _ = right[0].shape
        in_specs.append(
            pl.BlockSpec((peers, 1, slot_rows, tile), lambda n: (0, right_lane, 0, n))
        )
    operands += right
    if last:
        operands.append(near(base) if inside else base)
        in_specs.append(whole() if inside else column_block)
    if last:
        out_shape = jax.ShapeDtypeStruct((wide, out_cols), BF16)
    else:
        out_shape = (VMEM if inside else pltpu.HBM)((wide, out_cols), F32)
    return pl.pallas_call(
        body,
        grid=(out_cols // tile,),
        in_specs=in_specs,
        out_specs=whole() if inside and not last else column_block,
        out_shape=out_shape,
        scratch_shapes=[pltpu.VMEM((count, out_cols), BF16)] if pieces else [],
        compiler_params=params(24),
        name="outer_sum",
    )(*operands)


def dispatch(selector, x, peers):
    out = dot(selector, x).astype(BF16)
    return out.reshape(peers, 1, out.shape[0] // peers, out.shape[1])


def exchange(rows4):
    peers, lanes, slot_rows, cols = rows4.shape
    flat = rows4.reshape(peers, lanes * slot_rows, cols)
    got = lax.all_to_all(flat, "dict", split_axis=0, concat_axis=0, tiled=True)
    return got.reshape(rows4.shape)


def swap_pieces(pieces, size):
    out = [pieces[0]]
    for shift in range(1, size):
        out.append(lax.ppermute(pieces[shift], "dp", ring(size, shift)))
    return out


def total_of(refs):
    total = refs[0][...]
    for ref in refs[1:]:
        total = total + ref[...].astype(F32)
    return total


def activate(pieces, bias_enc):
    def body(*refs):
        gate_ref, act_ref = refs[-2:]
        gate = jnp.maximum(total_of(refs[:-3]) + refs[-3][...], 0.0)
        gate_ref[...] = gate
        act_ref[...] = (gate * gate).astype(BF16)

    shape = pieces[0].shape
    return pl.pallas_call(
        body,
        in_specs=[whole()] * (len(pieces) + 1),
        out_specs=[pl.BlockSpec(shape, lambda: (0, 0)), whole()],
        out_shape=[pltpu.HBM(shape, F32), jax.ShapeDtypeStruct(shape, BF16)],
        compiler_params=params(),
        name="activate",
    )(*pieces, bias_enc)


def grad_pre(pieces, gates, start):
    rows = pieces[0].shape[0]
    size = len(pieces)

    def body(*refs):
        total = total_of(refs[:size])
        done = 0
        for ref in refs[size:-1]:
            count = min(rows - done, ref.shape[0])
            part = total[done : done + count] * 2.0 * ref[pl.ds(start, count), :]
            refs[-1][pl.ds(done, count), :] = part.astype(BF16)
            done += count

    return pl.pallas_call(
        body,
        in_specs=[whole()] * (size + len(gates)),
        out_specs=whole(),
        out_shape=jax.ShapeDtypeStruct(pieces[0].shape, BF16),
        compiler_params=params(),
        name="grad_pre",
    )(*pieces, *gates)


def spread(own, size):
    out = [own]
    for shift in range(1, size):
        out.append(lax.ppermute(own, "dp", ring(size, shift)))
    return out


def on_device(acts, lists, w_enc, w_dec, b_enc, b_dec):
    peers = lax.axis_size("dict")
    size = lax.axis_size("dp")
    me = lax.axis_index("dp").reshape(1).astype(jnp.int32)
    block_count, active_count = lists.shape
    rows_block = acts.shape[0] // block_count
    cols = acts.shape[1]
    capacity = max(2, (2 * block_count * active_count + peers - 1) // peers)
    slot_total = peers * capacity
    sub = rows_block // CHUNKS
    slot_rows = capacity * sub

    flat_ids = lists.reshape(-1)
    onehot = (flat_ids[:, None] == jnp.arange(peers, dtype=jnp.int32)[None, :]).astype(jnp.int32)
    rank_index = jnp.sum((jnp.cumsum(onehot, axis=0) - 1) * onehot, axis=1)
    slot_index = flat_ids * capacity + rank_index
    item_block = jnp.arange(block_count * active_count, dtype=jnp.int32) // active_count
    hit = jnp.arange(slot_total, dtype=jnp.int32)[:, None] == slot_index[None, :]
    slot_block = jnp.sum(jnp.where(hit, item_block[None, :] + 1, 0), axis=1) - 1
    slot_row = slot_block[:, None] * sub + jnp.arange(sub, dtype=jnp.int32)[None, :]
    slot_row = jnp.where(slot_block[:, None] >= 0, slot_row, -1).reshape(-1)
    selector = (
        slot_row[:, None] == jnp.arange(block_count * sub, dtype=jnp.int32)[None, :]
    ).astype(BF16)

    blocks = acts.reshape(block_count, CHUNKS, sub, cols)
    x_a = blocks[:, 0].reshape(block_count * sub, cols)
    x_b = blocks[:, 1].reshape(block_count * sub, cols)
    bias_enc = b_enc.astype(F32).reshape(1, -1)
    bias_dec = b_dec.astype(F32).reshape(1, cols)
    scale = 1.0 / rows_block
    w_enc = far(w_enc)
    w_dec = far(w_dec)

    def share(rows4, lane, half, weight, transposed):
        return split_matmul(me, rows4, lane, half, weight, transposed, size)


    in_a = exchange(dispatch(selector, x_a, peers))
    in_b = exchange(after(dispatch(selector, x_b, peers), in_a))
    gates_a, own_a = [], []
    for h in range(2):
        pieces = share(in_a, 0, h, w_enc, False)
        pieces = swap_pieces(pieces, size)
        gate, act = activate(pieces, bias_enc)
        gates_a.append(gate)
        own_a.append(act)
    pieces_a = spread(own_a[0], size) + spread(own_a[1], size)
    enc_b = share(in_b, 0, None, w_enc, False)
    enc_b = swap_pieces(enc_b, size)
    part_a, act_a = decode(me, pieces_a, w_dec, peers, slot_rows, 1, 0, size)
    back_a = exchange(part_a)
    gate_b, own_b = activate(enc_b, bias_enc)
    pieces_b = spread(own_b, size)
    part_b, act_b = decode(me, pieces_b, w_dec, peers, slot_rows, 2, 0, size)
    mixed = residual_rows(selector, back_a, 0, x_a, bias_dec, scale, part_b, 1)
    mixed = far(exchange(mixed))
    resid_b = residual_rows(selector, mixed, 0, x_b, bias_dec, scale, None, 0)
    last = exchange(resid_b)
    back = share(mixed, 1, None, w_dec, True)
    back = swap_pieces(back, size)
    dec_sum = outer_sum(me, act_a, None, [mixed], 1, None, size, False)
    gp_a = grad_pre(back, gates_a, 0)
    pre_a = spread(gp_a, size)
    backs = []
    for h in range(2):
        pieces = share(last, 0, h, w_dec, True)
        backs.append(swap_pieces(pieces, size))
    enc_sum = outer_sum(me, in_a, 0, pre_a, None, None, size, True)
    half = gate_b.shape[0] // 2
    pre_b = []
    for h in range(2):
        pieces = backs[h]
        if h == 0:
            pieces[0] = after(pieces[0], enc_sum)
        gp_b = grad_pre(pieces, [gate_b], h * half)
        pre_b += spread(gp_b, size)
    grad_dec = outer_sum(me, act_b, None, [last], 0, dec_sum, size, False)
    grad_enc = outer_sum(me, in_b, 0, pre_b, None, enc_sum, size, True)
    return grad_enc, grad_dec


def solution(mesh):
    in_specs = (
        P("dict", "dp"),
        P("dict", None),
        P("dp", "dict"),
        P("dict", "dp"),
        P("dict"),
        P("dp"),
    )
    out_specs = (P("dp", "dict"), P("dict", "dp"))
    return jax.shard_map(
        on_device, mesh=mesh, in_specs=in_specs, out_specs=out_specs, check_vma=False
    )
```

```python
import jax
import jax.numpy as jnp
from jax import lax
from jax.experimental import pallas as pl
from jax.experimental.pallas import tpu as pltpu
from jax.sharding import PartitionSpec as P


CHUNKS = 2
F32 = jnp.float32
BF16 = jnp.bfloat16
VMEM = pltpu.VMEM


def dot(a, b, dims=((1,), (0,))):
    return lax.dot_general(a, b, (dims, ((), ())), preferred_element_type=F32)


def after(value, *others):
    return lax.optimization_barrier((value,) + others)[0]


def ring(size, shift):
    return [(i, (i + shift) % size) for i in range(size)]


def params(mib=12):
    return pltpu.CompilerParams(vmem_limit_bytes=mib * 1024 * 1024)


def near(value):
    return pltpu.with_memory_space_constraint(value, VMEM)


def far(value):
    return pltpu.with_memory_space_constraint(value, pltpu.HBM)


def whole():
    return pl.BlockSpec(memory_space=VMEM)


def split_matmul(me, rows4, lane, half, weight, transposed, size, tile=512, keep=False, kept=False, away=False):
    peers, _, slot_rows, inner = rows4.shape
    halves = 2 if half is None else 1
    my_peers = peers * halves // 2
    first = 0 if half is None else half * my_peers
    count = my_peers * slot_rows
    quarter = count // (size * halves)
    if kept:
        tiles = weight.shape
        outer = tiles[0] * (tiles[1] if transposed else tiles[2])
    else:
        outer = weight.shape[0] if transposed else weight.shape[1]
        tiles = (outer // tile, tile, inner) if transposed else (outer // tile, inner, tile)
    tile = outer // tiles[0]

    def body(me_ref, x_any, w_any, *rest):
        own_ref, sends, rest = rest[0], rest[1:size], rest[size:]
        if keep:
            w_ref, rest = rest[0], rest[1:]
        if kept:
            w_ref = w_any
        acc, x_ref, x_sem = rest[:3]
        if not (keep or kept):
            w_ref = rest[3]
        w_sem = rest[-1]

        def fetch(n):
            cols = pl.ds(n * tile, tile)
            source = w_any.at[cols, :] if transposed else w_any.at[:, cols]
            return pltpu.make_async_copy(source, w_ref.at[n], w_sem.at[n])

        x_copy = pltpu.make_async_copy(x_any.at[pl.ds(first, my_peers), lane], x_ref, x_sem)
        x_copy.start()
        if not kept:
            for n in range(tiles[0]):
                fetch(n).start()
        x_copy.wait()

        for n in range(tiles[0]):
            if not kept:
                fetch(n).wait()
            rows = x_ref[...].reshape(count, inner)
            dims = ((1,), (1,)) if transposed else ((1,), (0,))
            acc[:, n * tile : (n + 1) * tile] = dot(rows, w_ref[n], dims)

        mine = me_ref[0]
        for h in range(halves):
            to = pl.ds(h * quarter, quarter)

            def piece(index):
                start = pl.multiple_of((index + h * size) * quarter, quarter)
                return acc[pl.ds(start, quarter), :]

            own_ref[to, :] = piece(mine)
            for shift in range(1, size):
                sends[shift - 1][to, :] = piece(lax.rem(mine + shift, size)).astype(BF16)

    return pl.pallas_call(
        body,
        in_specs=[
            pl.BlockSpec(memory_space=pltpu.SMEM),
            pl.BlockSpec(memory_space=pl.ANY),
            whole() if kept else pl.BlockSpec(memory_space=pltpu.HBM),
        ],
        out_specs=[pl.BlockSpec((halves * quarter, outer), lambda: (0, 0)) if away else whole()]
        + [whole()] * (size - 1 + (1 if keep else 0)),
        out_shape=[(pltpu.HBM if away else jax.ShapeDtypeStruct)((halves * quarter, outer), F32)]
        + [jax.ShapeDtypeStruct((halves * quarter, outer), BF16)] * (size - 1)
        + ([VMEM(tiles, BF16)] if keep else []),
        scratch_shapes=[
            pltpu.VMEM((count, outer), F32),
            pltpu.VMEM((my_peers, slot_rows, inner), BF16),
            pltpu.SemaphoreType.DMA,
        ]
        + ([] if keep or kept else [pltpu.VMEM(tiles, BF16)])
        + ([] if kept else [pltpu.SemaphoreType.DMA((tiles[0],))]),
        compiler_params=params(20),
        name="split_matmul",
    )(me, rows4, near(weight) if kept else weight)


def assemble(me, parts, out_ref, size):
    quarter = out_ref.shape[0] // (2 * size)
    for i, part in enumerate(parts):
        owner = lax.rem(me + size - i % size, size)
        for j in range(part.shape[0] // quarter):
            index = owner + (i // size + j) * size
            to = pl.ds(pl.multiple_of(index * quarter, quarter), quarter)
            out_ref[to, :] = part[pl.ds(j * quarter, quarter), :]


def decode(me, pieces, w_dec, peers, slot_rows, lanes, lane, size):
    count = peers * slot_rows
    inner, outer = w_dec.shape
    tile = 1024

    def body(me_ref, *refs):
        parts, w_ref, out_ref, act_ref = refs[:-3], refs[-3], refs[-2], refs[-1]
        step = pl.program_id(0)

        @pl.when(step == 0)
        def _():
            assemble(me_ref[0], parts, act_ref, size)

        part = dot(act_ref[...], w_ref[...]).astype(BF16)
        out_ref[...] = part.reshape(peers, 1, slot_rows, tile)

    return pl.pallas_call(
        body,
        grid=(outer // tile,),
        in_specs=[pl.BlockSpec(memory_space=pltpu.SMEM)]
        + [whole()] * len(pieces)
        + [pl.BlockSpec((inner, tile), lambda n: (0, n))],
        out_specs=[
            pl.BlockSpec((peers, 1, slot_rows, tile), lambda n: (0, lane, 0, n)),
            pl.BlockSpec((count, inner), lambda n: (0, 0)),
        ],
        out_shape=[
            pltpu.HBM((peers, lanes, slot_rows, outer), BF16),
            pltpu.HBM((count, inner), BF16),
        ],
        compiler_params=params(24),
        name="decode",
    )(me, *pieces, w_dec)


def residual_rows(selector, returned, lane, blocks, chunk, bias_dec, scale, target, target_lane):
    peers, _, slot_rows, cols = returned.shape
    count = peers * slot_rows
    home = selector.shape[1]
    block_count, rows_block, _ = blocks.shape
    tile = 1024

    def body(sel_ref, got_ref, x_ref, b_ref, *rest):
        out_ref = rest[-1]
        sel = sel_ref[...]
        rebuilt = dot(sel, got_ref[...].reshape(count, tile), ((0,), (0,))) + b_ref[...]
        rows = x_ref[...].reshape(home, tile)
        residual = ((rebuilt - rows.astype(F32)) * scale).astype(BF16)
        out_ref[...] = dot(sel, residual).astype(BF16).reshape(peers, 1, slot_rows, tile)

    in_specs = [
        whole(),
        pl.BlockSpec((peers, 1, slot_rows, tile), lambda n: (0, lane, 0, n)),
        pl.BlockSpec((block_count, rows_block // CHUNKS, tile), lambda n: (0, chunk, n)),
        pl.BlockSpec((1, tile), lambda n: (0, n)),
    ]
    operands = [selector, returned, blocks, bias_dec]
    aliases = {}
    lanes = 1
    if target is not None:
        in_specs.append(pl.BlockSpec(memory_space=pltpu.HBM))
        operands.append(target)
        aliases = {4: 0}
        lanes = target.shape[1]
    return pl.pallas_call(
        body,
        grid=(cols // tile,),
        in_specs=in_specs,
        out_specs=pl.BlockSpec((peers, 1, slot_rows, tile), lambda n: (0, target_lane, 0, n)),
        out_shape=pltpu.HBM((peers, lanes, slot_rows, cols), BF16),
        input_output_aliases=aliases,
        compiler_params=params(24),
        name="residual_rows",
    )(*operands)


def outer_sum(me, left, left_lane, right, right_lane, base, size, inside):
    pieces = right_lane is None
    if left_lane is None:
        count, wide = left.shape
    else:
        count, wide = left.shape[0] * left.shape[2], left.shape[3]
    out_cols = right[0].shape[-1]
    last = base is not None
    tile = 512 if last and inside else 1024

    def body(me_ref, left_ref, *refs):
        right_refs = refs[: len(right)]
        out_ref = refs[len(right) + (1 if last else 0)]
        step = pl.program_id(0)
        here = pl.ds(pl.multiple_of(step * tile, tile), tile)
        lhs = left_ref[...].reshape(count, wide)
        if pieces:
            rows_ref = refs[-1]

            @pl.when(step == 0)
            def _():
                assemble(me_ref[0], right_refs, rows_ref, size)

            rhs = rows_ref[:, here]
        else:
            rhs = right_refs[0][...].reshape(count, tile)
        total = dot(lhs, rhs, ((0,), (0,)))
        if last:
            base_ref = refs[len(right)]
            out_ref[...] = (total + base_ref[:, here]).astype(BF16)
        elif inside:
            out_ref[:, here] = total
        else:
            out_ref[...] = total

    column_block = pl.BlockSpec((wide, tile), lambda n: (0, n))
    in_specs = [pl.BlockSpec(memory_space=pltpu.SMEM)]
    operands = [me, left]
    if left_lane is None:
        in_specs.append(pl.BlockSpec((count, wide), lambda n: (0, 0)))
    else:
        operands[1] = near(left)
        in_specs.append(whole())
    if pieces:
        in_specs += [whole()] * len(right)
    else:
        peers, _, slot_rows, _ = right[0].shape
        in_specs.append(
            pl.BlockSpec((peers, 1, slot_rows, tile), lambda n: (0, right_lane, 0, n))
        )
    operands += right
    if last:
        operands.append(near(base))
        in_specs.append(whole())
    if last:
        out_shape = jax.ShapeDtypeStruct((wide, out_cols), BF16)
    else:
        out_shape = (VMEM if inside else pltpu.HBM)((wide, out_cols), F32)
    return pl.pallas_call(
        body,
        grid=(out_cols // tile,),
        in_specs=in_specs,
        out_specs=whole() if inside and not last else column_block,
        out_shape=out_shape,
        scratch_shapes=[pltpu.VMEM((count, out_cols), BF16)] if pieces else [],
        compiler_params=params(22 if last else 30),
        name="outer_sum",
    )(*operands)


def encoder_sum(me, left, pieces, base, size):
    peers, _, slot_rows, wide = left.shape
    count = peers * slot_rows
    cols = pieces[0].shape[1]
    tile = 512

    def body(me_ref, left_ref, *refs):
        rows_ref = refs[-1]
        step = pl.program_id(0)
        here = pl.ds(pl.multiple_of(step * tile, tile), tile)

        @pl.when(step == 0)
        def _():
            assemble(me_ref[0], refs[: len(pieces)], rows_ref, size)

        lhs = left_ref[...].reshape(count, tile)
        total = dot(lhs, rows_ref[...], ((0,), (0,)))
        refs[-2][...] = (total + refs[-3][here, :]).astype(BF16)

    return pl.pallas_call(
        body,
        grid=(wide // tile,),
        in_specs=[
            pl.BlockSpec(memory_space=pltpu.SMEM),
            pl.BlockSpec((peers, 1, slot_rows, tile), lambda n: (0, 0, 0, n)),
        ]
        + [whole()] * (len(pieces) + 1),
        out_specs=pl.BlockSpec((tile, cols), lambda n: (n, 0)),
        out_shape=jax.ShapeDtypeStruct((wide, cols), BF16),
        scratch_shapes=[pltpu.VMEM((count, cols), BF16)],
        compiler_params=params(20),
        name="encoder_sum",
    )(me, left, *pieces, near(base))


def dispatch(selector, blocks, chunk, peers):
    count, home = selector.shape
    block_count, rows_block, cols = blocks.shape
    sub = rows_block // CHUNKS
    tile = 1024

    def body(sel_ref, x_ref, out_ref):
        out = dot(sel_ref[...], x_ref[...].reshape(home, tile)).astype(BF16)
        out_ref[...] = out.reshape(out_ref.shape)

    return pl.pallas_call(
        body,
        grid=(cols // tile,),
        in_specs=[
            whole(),
            pl.BlockSpec((block_count, sub, tile), lambda n: (0, chunk, n)),
        ],
        out_specs=pl.BlockSpec((peers, 1, count // peers, tile), lambda n: (0, 0, 0, n)),
        out_shape=pltpu.HBM((peers, 1, count // peers, cols), BF16),
        compiler_params=params(),
        name="dispatch",
    )(selector, blocks)


def exchange(rows4):
    peers, lanes, slot_rows, cols = rows4.shape
    flat = rows4.reshape(peers, lanes * slot_rows, cols)
    got = lax.all_to_all(flat, "dict", split_axis=0, concat_axis=0, tiled=True)
    return got.reshape(rows4.shape)


def swap_pieces(pieces, size):
    out = [pieces[0]]
    for shift in range(1, size):
        out.append(lax.ppermute(pieces[shift], "dp", ring(size, shift)))
    return out


def total_of(refs):
    total = refs[0][...]
    for ref in refs[1:]:
        total = total + ref[...].astype(F32)
    return total


def activate(pieces, bias_enc):
    def body(*refs):
        gate_ref, act_ref = refs[-2:]
        gate = jnp.maximum(total_of(refs[:-3]) + refs[-3][...], 0.0)
        gate_ref[...] = gate
        act_ref[...] = (gate * gate).astype(BF16)

    shape = pieces[0].shape
    return pl.pallas_call(
        body,
        in_specs=[whole()] * (len(pieces) + 1),
        out_specs=[pl.BlockSpec(shape, lambda: (0, 0)), whole()],
        out_shape=[pltpu.HBM(shape, F32), jax.ShapeDtypeStruct(shape, BF16)],
        compiler_params=params(),
        name="activate",
    )(*pieces, bias_enc)


def grad_pre(pieces, gates, start):
    rows = pieces[0].shape[0]
    size = len(pieces)

    def body(*refs):
        total = total_of(refs[:size])
        done = 0
        for ref in refs[size:-1]:
            count = min(rows - done, ref.shape[0])
            part = total[done : done + count] * 2.0 * ref[pl.ds(start, count), :]
            refs[-1][pl.ds(done, count), :] = part.astype(BF16)
            done += count

    return pl.pallas_call(
        body,
        in_specs=[whole()] * (size + len(gates)),
        out_specs=whole(),
        out_shape=jax.ShapeDtypeStruct(pieces[0].shape, BF16),
        compiler_params=params(),
        name="grad_pre",
    )(*pieces, *gates)


def spread(own, size):
    out = [own]
    for shift in range(1, size):
        out.append(lax.ppermute(own, "dp", ring(size, shift)))
    return out


def on_device(acts, lists, w_enc, w_dec, b_enc, b_dec):
    peers = lax.axis_size("dict")
    size = lax.axis_size("dp")
    me = lax.axis_index("dp").reshape(1).astype(jnp.int32)
    block_count, active_count = lists.shape
    rows_block = acts.shape[0] // block_count
    cols = acts.shape[1]
    capacity = max(2, (2 * block_count * active_count + peers - 1) // peers)
    slot_total = peers * capacity
    sub = rows_block // CHUNKS
    slot_rows = capacity * sub

    flat_ids = lists.reshape(-1)
    onehot = (flat_ids[:, None] == jnp.arange(peers, dtype=jnp.int32)[None, :]).astype(jnp.int32)
    rank_index = jnp.sum((jnp.cumsum(onehot, axis=0) - 1) * onehot, axis=1)
    slot_index = flat_ids * capacity + rank_index
    item_block = jnp.arange(block_count * active_count, dtype=jnp.int32) // active_count
    hit = jnp.arange(slot_total, dtype=jnp.int32)[:, None] == slot_index[None, :]
    slot_block = jnp.sum(jnp.where(hit, item_block[None, :] + 1, 0), axis=1) - 1
    slot_row = slot_block[:, None] * sub + jnp.arange(sub, dtype=jnp.int32)[None, :]
    slot_row = jnp.where(slot_block[:, None] >= 0, slot_row, -1).reshape(-1)
    selector = (
        slot_row[:, None] == jnp.arange(block_count * sub, dtype=jnp.int32)[None, :]
    ).astype(BF16)

    blocks = acts.reshape(block_count, rows_block, cols)
    bias_enc = b_enc.astype(F32).reshape(1, -1)
    bias_dec = b_dec.astype(F32).reshape(1, cols)
    scale = 1.0 / rows_block
    w_enc = far(w_enc)
    w_dec = far(w_dec)

    def share(rows4, lane, weight, transposed, away=False):
        return split_matmul(me, rows4, lane, None, weight, transposed, size, away=away)

    def first_half(rows4, weight, transposed):
        *pieces, tiles = split_matmul(me, rows4, 0, 0, weight, transposed, size, keep=True)
        return pieces, tiles

    def second_half(rows4, tiles, transposed):
        return split_matmul(me, rows4, 0, 1, tiles, transposed, size, kept=True)


    in_a = exchange(dispatch(selector, blocks, 0, peers))
    in_b = exchange(after(dispatch(selector, blocks, 1, peers), in_a))
    gates_a, own_a = [], []
    for h in range(2):
        if h == 0:
            pieces, tiles = first_half(in_a, w_enc, False)
        else:
            pieces = second_half(in_a, tiles, False)
        pieces = swap_pieces(pieces, size)
        gate, act = activate(pieces, bias_enc)
        gates_a.append(gate)
        own_a.append(act)
    pieces_a = spread(own_a[0], size) + spread(own_a[1], size)
    enc_b = share(in_b, 0, w_enc, False, True)
    enc_b = swap_pieces(enc_b, size)
    part_a, act_a = decode(me, pieces_a, w_dec, peers, slot_rows, 1, 0, size)
    back_a = exchange(part_a)
    gate_b, own_b = activate(enc_b, bias_enc)
    pieces_b = spread(own_b, size)
    part_b, act_b = decode(me, pieces_b, w_dec, peers, slot_rows, 2, 0, size)
    mixed = residual_rows(selector, back_a, 0, blocks, 0, bias_dec, scale, part_b, 1)
    mixed = far(exchange(mixed))
    resid_b = residual_rows(selector, mixed, 0, blocks, 1, bias_dec, scale, None, 0)
    last = exchange(resid_b)
    back = share(mixed, 1, w_dec, True)
    back = swap_pieces(back, size)
    dec_sum = outer_sum(me, act_a, None, [mixed], 1, None, size, False)
    gp_a = grad_pre(back, gates_a, 0)
    pre_a = spread(gp_a, size)
    backs = []
    for h in range(2):
        if h == 0:
            pieces, tiles = first_half(last, w_dec, True)
        else:
            pieces = second_half(last, tiles, True)
        backs.append(swap_pieces(pieces, size))
    enc_sum = outer_sum(me, in_a, 0, pre_a, None, None, size, True)
    half = gate_b.shape[0] // 2
    pre_b = []
    for h in range(2):
        pieces = backs[h]
        if h == 0:
            pieces[0] = after(pieces[0], enc_sum)
        gp_b = grad_pre(pieces, [gate_b], h * half)
        pre_b += spread(gp_b, size)
    grad_dec = outer_sum(me, act_b, None, [last], 0, dec_sum, size, False)
    grad_enc = encoder_sum(me, in_b, pre_b, enc_sum, size)
    return grad_enc, grad_dec


def solution(mesh):
    in_specs = (
        P("dict", "dp"),
        P("dict", None),
        P("dp", "dict"),
        P("dict", "dp"),
        P("dict"),
        P("dp"),
    )
    out_specs = (P("dp", "dict"), P("dict", "dp"))
    return jax.shard_map(
        on_device, mesh=mesh, in_specs=in_specs, out_specs=out_specs, check_vma=False
    )
```

```python
import jax
import jax.numpy as jnp
from jax import lax
from jax.experimental import pallas as pl
from jax.experimental.pallas import tpu as pltpu
from jax.sharding import PartitionSpec as P


CHUNKS = 2
F32 = jnp.float32
BF16 = jnp.bfloat16
VMEM = pltpu.VMEM


def dot(a, b, dims=((1,), (0,))):
    return lax.dot_general(a, b, (dims, ((), ())), preferred_element_type=F32)


def after(value, *others):
    return lax.optimization_barrier((value,) + others)[0]


def ring(size, shift):
    return [(i, (i + shift) % size) for i in range(size)]


def params(mib=12):
    return pltpu.CompilerParams(vmem_limit_bytes=mib * 1024 * 1024)


def near(value):
    return pltpu.with_memory_space_constraint(value, VMEM)


def far(value):
    return pltpu.with_memory_space_constraint(value, pltpu.HBM)


def whole():
    return pl.BlockSpec(memory_space=VMEM)


def split_matmul(me, rows4, lane, half, weight, transposed, size, tile=512, keep=False, kept=False, away=False):
    peers, _, slot_rows, inner = rows4.shape
    halves = 2 if half is None else 1
    my_peers = peers * halves // 2
    first = 0 if half is None else half * my_peers
    count = my_peers * slot_rows
    quarter = count // (size * halves)
    if kept:
        tiles = weight.shape
        outer = tiles[0] * (tiles[1] if transposed else tiles[2])
    else:
        outer = weight.shape[0] if transposed else weight.shape[1]
        tiles = (outer // tile, tile, inner) if transposed else (outer // tile, inner, tile)
    tile = outer // tiles[0]

    def body(me_ref, x_any, w_any, *rest):
        own_ref, sends, rest = rest[0], rest[1:size], rest[size:]
        if keep:
            w_ref, rest = rest[0], rest[1:]
        if kept:
            w_ref = w_any
        acc, x_ref, x_sem = rest[:3]
        if not (keep or kept):
            w_ref = rest[3]
        w_sem = rest[-1]

        def fetch(n):
            cols = pl.ds(n * tile, tile)
            source = w_any.at[cols, :] if transposed else w_any.at[:, cols]
            return pltpu.make_async_copy(source, w_ref.at[n], w_sem.at[n])

        x_copy = pltpu.make_async_copy(x_any.at[pl.ds(first, my_peers), lane], x_ref, x_sem)
        x_copy.start()
        if not kept:
            for n in range(tiles[0]):
                fetch(n).start()
        x_copy.wait()

        for n in range(tiles[0]):
            if not kept:
                fetch(n).wait()
            rows = x_ref[...].reshape(count, inner)
            dims = ((1,), (1,)) if transposed else ((1,), (0,))
            acc[:, n * tile : (n + 1) * tile] = dot(rows, w_ref[n], dims)

        mine = me_ref[0]
        for h in range(halves):
            to = pl.ds(h * quarter, quarter)

            def piece(index):
                start = pl.multiple_of((index + h * size) * quarter, quarter)
                return acc[pl.ds(start, quarter), :]

            own_ref[to, :] = piece(mine)
            for shift in range(1, size):
                sends[shift - 1][to, :] = piece(lax.rem(mine + shift, size)).astype(BF16)

    return pl.pallas_call(
        body,
        in_specs=[
            pl.BlockSpec(memory_space=pltpu.SMEM),
            pl.BlockSpec(memory_space=pl.ANY),
            whole() if kept else pl.BlockSpec(memory_space=pltpu.HBM),
        ],
        out_specs=[pl.BlockSpec((halves * quarter, outer), lambda: (0, 0)) if away else whole()]
        + [whole()] * (size - 1 + (1 if keep else 0)),
        out_shape=[(pltpu.HBM if away else jax.ShapeDtypeStruct)((halves * quarter, outer), F32)]
        + [jax.ShapeDtypeStruct((halves * quarter, outer), BF16)] * (size - 1)
        + ([VMEM(tiles, BF16)] if keep else []),
        scratch_shapes=[
            pltpu.VMEM((count, outer), F32),
            pltpu.VMEM((my_peers, slot_rows, inner), BF16),
            pltpu.SemaphoreType.DMA,
        ]
        + ([] if keep or kept else [pltpu.VMEM(tiles, BF16)])
        + ([] if kept else [pltpu.SemaphoreType.DMA((tiles[0],))]),
        compiler_params=params(20),
        name="split_matmul",
    )(me, rows4, near(weight) if kept else weight)


def assemble(me, parts, out_ref, size):
    quarter = out_ref.shape[0] // (2 * size)
    for i, part in enumerate(parts):
        owner = lax.rem(me + size - i % size, size)
        for j in range(part.shape[0] // quarter):
            index = owner + (i // size + j) * size
            to = pl.ds(pl.multiple_of(index * quarter, quarter), quarter)
            out_ref[to, :] = part[pl.ds(j * quarter, quarter), :]


def decode(me, pieces, w_dec, peers, slot_rows, lanes, lane, size):
    count = peers * slot_rows
    inner, outer = w_dec.shape
    tile = 1024

    def body(me_ref, *refs):
        parts, w_ref, out_ref, act_ref = refs[:-3], refs[-3], refs[-2], refs[-1]
        step = pl.program_id(0)

        @pl.when(step == 0)
        def _():
            assemble(me_ref[0], parts, act_ref, size)

        part = dot(act_ref[...], w_ref[...]).astype(BF16)
        out_ref[...] = part.reshape(peers, 1, slot_rows, tile)

    return pl.pallas_call(
        body,
        grid=(outer // tile,),
        in_specs=[pl.BlockSpec(memory_space=pltpu.SMEM)]
        + [whole()] * len(pieces)
        + [pl.BlockSpec((inner, tile), lambda n: (0, n))],
        out_specs=[
            pl.BlockSpec((peers, 1, slot_rows, tile), lambda n: (0, lane, 0, n)),
            pl.BlockSpec((count, inner), lambda n: (0, 0)),
        ],
        out_shape=[
            pltpu.HBM((peers, lanes, slot_rows, outer), BF16),
            pltpu.HBM((count, inner), BF16),
        ],
        compiler_params=params(24),
        name="decode",
    )(me, *pieces, w_dec)


def residual_rows(selector, returned, lane, blocks, chunk, bias_dec, scale, target, target_lane):
    peers, _, slot_rows, cols = returned.shape
    count = peers * slot_rows
    home = selector.shape[1]
    block_count, rows_block, _ = blocks.shape
    tile = 1024

    def body(sel_ref, got_ref, x_ref, b_ref, *rest):
        out_ref = rest[-1]
        sel = sel_ref[...]
        rebuilt = dot(sel, got_ref[...].reshape(count, tile), ((0,), (0,))) + b_ref[...]
        rows = x_ref[...].reshape(home, tile)
        residual = ((rebuilt - rows.astype(F32)) * scale).astype(BF16)
        out_ref[...] = dot(sel, residual).astype(BF16).reshape(peers, 1, slot_rows, tile)

    in_specs = [
        whole(),
        pl.BlockSpec((peers, 1, slot_rows, tile), lambda n: (0, lane, 0, n)),
        pl.BlockSpec((block_count, rows_block // CHUNKS, tile), lambda n: (0, chunk, n)),
        pl.BlockSpec((1, tile), lambda n: (0, n)),
    ]
    operands = [selector, returned, blocks, bias_dec]
    aliases = {}
    lanes = 1
    if target is not None:
        in_specs.append(pl.BlockSpec(memory_space=pltpu.HBM))
        operands.append(target)
        aliases = {4: 0}
        lanes = target.shape[1]
    return pl.pallas_call(
        body,
        grid=(cols // tile,),
        in_specs=in_specs,
        out_specs=pl.BlockSpec((peers, 1, slot_rows, tile), lambda n: (0, target_lane, 0, n)),
        out_shape=pltpu.HBM((peers, lanes, slot_rows, cols), BF16),
        input_output_aliases=aliases,
        compiler_params=params(24),
        name="residual_rows",
    )(*operands)


def outer_sum(me, left, left_lane, right, right_lane, base, size, inside, carry=None):
    pieces = right_lane is None
    if left_lane is None:
        count, wide = left.shape
    else:
        count, wide = left.shape[0] * left.shape[2], left.shape[3]
    out_cols = right[0].shape[-1]
    last = base is not None
    tile = 512 if last and inside else 1024

    def body(me_ref, left_ref, *refs):
        right_refs = refs[: len(right)]
        out_ref = refs[len(right) + (1 if last or carry is not None else 0)]
        step = pl.program_id(0)
        if carry is not None:
            copy = pltpu.make_async_copy(refs[len(right)], refs[len(right) + 2], refs[-1])
            copy.start()
        here = pl.ds(pl.multiple_of(step * tile, tile), tile)
        lhs = left_ref[...].reshape(count, wide)
        if pieces:
            rows_ref = refs[-1 if carry is None else -2]

            @pl.when(step == 0)
            def _():
                assemble(me_ref[0], right_refs, rows_ref, size)

            rhs = rows_ref[:, here]
        else:
            rhs = right_refs[0][...].reshape(count, tile)
        total = dot(lhs, rhs, ((0,), (0,)))
        if last:
            base_ref = refs[len(right)]
            out_ref[...] = (total + base_ref[:, here]).astype(BF16)
        elif inside:
            out_ref[:, here] = total
        else:
            out_ref[...] = total
        if carry is not None:
            copy.wait()

    column_block = pl.BlockSpec((wide, tile), lambda n: (0, n))
    in_specs = [pl.BlockSpec(memory_space=pltpu.SMEM)]
    operands = [me, left]
    if left_lane is None:
        in_specs.append(pl.BlockSpec((count, wide), lambda n: (0, 0)))
    else:
        operands[1] = near(left)
        in_specs.append(whole())
    if pieces:
        in_specs += [whole()] * len(right)
    else:
        peers, _, slot_rows, _ = right[0].shape
        in_specs.append(
            pl.BlockSpec((peers, 1, slot_rows, tile), lambda n: (0, right_lane, 0, n))
        )
    operands += right
    if last:
        operands.append(near(base))
        in_specs.append(whole())
    if last:
        out_shape = jax.ShapeDtypeStruct((wide, out_cols), BF16)
    else:
        out_shape = (VMEM if inside else pltpu.HBM)((wide, out_cols), F32)
    out_specs = whole() if inside and not last else column_block
    scratch = [pltpu.VMEM((count, out_cols), BF16)] if pieces else []
    if carry is not None:
        assert out_cols == tile
        operands.append(carry)
        in_specs.append(pl.BlockSpec(memory_space=pl.ANY))
        out_shape = [out_shape, VMEM(carry.shape, carry.dtype)]
        out_specs = [out_specs, whole()]
        scratch.append(pltpu.SemaphoreType.DMA)
    return pl.pallas_call(
        body,
        grid=(out_cols // tile,),
        in_specs=in_specs,
        out_specs=out_specs,
        out_shape=out_shape,
        scratch_shapes=scratch,
        compiler_params=params(22 if last else 30),
        name="outer_sum",
    )(*operands)


def encoder_sum(me, left, pieces, base, size):
    peers, _, slot_rows, wide = left.shape
    count = peers * slot_rows
    cols = pieces[0].shape[1]
    tile = 512

    def body(me_ref, left_ref, *refs):
        rows_ref = refs[-1]
        step = pl.program_id(0)
        here = pl.ds(pl.multiple_of(step * tile, tile), tile)

        @pl.when(step == 0)
        def _():
            assemble(me_ref[0], refs[: len(pieces)], rows_ref, size)

        lhs = left_ref[:, 0, :, here].reshape(count, tile)
        total = dot(lhs, rows_ref[...], ((0,), (0,)))
        refs[-2][...] = (total + refs[-3][here, :]).astype(BF16)

    return pl.pallas_call(
        body,
        grid=(wide // tile,),
        in_specs=[
            pl.BlockSpec(memory_space=pltpu.SMEM),
            whole(),
        ]
        + [whole()] * (len(pieces) + 1),
        out_specs=pl.BlockSpec((tile, cols), lambda n: (n, 0)),
        out_shape=jax.ShapeDtypeStruct((wide, cols), BF16),
        scratch_shapes=[pltpu.VMEM((count, cols), BF16)],
        compiler_params=params(20),
        name="encoder_sum",
    )(me, near(left), *pieces, near(base))


def dispatch(selector, blocks, chunk, peers):
    count, home = selector.shape
    block_count, rows_block, cols = blocks.shape
    sub = rows_block // CHUNKS
    tile = 1024

    def body(sel_ref, x_ref, out_ref):
        out = dot(sel_ref[...], x_ref[...].reshape(home, tile)).astype(BF16)
        out_ref[...] = out.reshape(out_ref.shape)

    return pl.pallas_call(
        body,
        grid=(cols // tile,),
        in_specs=[
            whole(),
            pl.BlockSpec((block_count, sub, tile), lambda n: (0, chunk, n)),
        ],
        out_specs=pl.BlockSpec((peers, 1, count // peers, tile), lambda n: (0, 0, 0, n)),
        out_shape=pltpu.HBM((peers, 1, count // peers, cols), BF16),
        compiler_params=params(),
        name="dispatch",
    )(selector, blocks)


def exchange(rows4):
    peers, lanes, slot_rows, cols = rows4.shape
    flat = rows4.reshape(peers, lanes * slot_rows, cols)
    got = lax.all_to_all(flat, "dict", split_axis=0, concat_axis=0, tiled=True)
    return got.reshape(rows4.shape)


def swap_pieces(pieces, size):
    out = [pieces[0]]
    for shift in range(1, size):
        out.append(lax.ppermute(pieces[shift], "dp", ring(size, shift)))
    return out


def total_of(refs):
    total = refs[0][...]
    for ref in refs[1:]:
        total = total + ref[...].astype(F32)
    return total


def activate(pieces, bias_enc):
    def body(*refs):
        gate_ref, act_ref = refs[-2:]
        gate = jnp.maximum(total_of(refs[:-3]) + refs[-3][...], 0.0)
        gate_ref[...] = gate
        act_ref[...] = (gate * gate).astype(BF16)

    shape = pieces[0].shape
    return pl.pallas_call(
        body,
        in_specs=[whole()] * (len(pieces) + 1),
        out_specs=[pl.BlockSpec(shape, lambda: (0, 0)), whole()],
        out_shape=[pltpu.HBM(shape, F32), jax.ShapeDtypeStruct(shape, BF16)],
        compiler_params=params(),
        name="activate",
    )(*pieces, bias_enc)


def grad_pre(pieces, gates, start):
    rows = pieces[0].shape[0]
    size = len(pieces)

    def body(*refs):
        total = total_of(refs[:size])
        done = 0
        for ref in refs[size:-1]:
            count = min(rows - done, ref.shape[0])
            part = total[done : done + count] * 2.0 * ref[pl.ds(start, count), :]
            refs[-1][pl.ds(done, count), :] = part.astype(BF16)
            done += count

    return pl.pallas_call(
        body,
        in_specs=[whole()] * (size + len(gates)),
        out_specs=whole(),
        out_shape=jax.ShapeDtypeStruct(pieces[0].shape, BF16),
        compiler_params=params(),
        name="grad_pre",
    )(*pieces, *gates)


def spread(own, size):
    out = [own]
    for shift in range(1, size):
        out.append(lax.ppermute(own, "dp", ring(size, shift)))
    return out


def on_device(acts, lists, w_enc, w_dec, b_enc, b_dec):
    peers = lax.axis_size("dict")
    size = lax.axis_size("dp")
    me = lax.axis_index("dp").reshape(1).astype(jnp.int32)
    block_count, active_count = lists.shape
    rows_block = acts.shape[0] // block_count
    cols = acts.shape[1]
    capacity = max(2, (2 * block_count * active_count + peers - 1) // peers)
    slot_total = peers * capacity
    sub = rows_block // CHUNKS
    slot_rows = capacity * sub

    flat_ids = lists.reshape(-1)
    onehot = (flat_ids[:, None] == jnp.arange(peers, dtype=jnp.int32)[None, :]).astype(jnp.int32)
    rank_index = jnp.sum((jnp.cumsum(onehot, axis=0) - 1) * onehot, axis=1)
    slot_index = flat_ids * capacity + rank_index
    item_block = jnp.arange(block_count * active_count, dtype=jnp.int32) // active_count
    hit = jnp.arange(slot_total, dtype=jnp.int32)[:, None] == slot_index[None, :]
    slot_block = jnp.sum(jnp.where(hit, item_block[None, :] + 1, 0), axis=1) - 1
    slot_row = slot_block[:, None] * sub + jnp.arange(sub, dtype=jnp.int32)[None, :]
    slot_row = jnp.where(slot_block[:, None] >= 0, slot_row, -1).reshape(-1)
    selector = (
        slot_row[:, None] == jnp.arange(block_count * sub, dtype=jnp.int32)[None, :]
    ).astype(BF16)

    blocks = acts.reshape(block_count, rows_block, cols)
    bias_enc = b_enc.astype(F32).reshape(1, -1)
    bias_dec = b_dec.astype(F32).reshape(1, cols)
    scale = 1.0 / rows_block
    w_enc = far(w_enc)
    w_dec = far(w_dec)

    def share(rows4, lane, weight, transposed, away=False):
        return split_matmul(me, rows4, lane, None, weight, transposed, size, away=away)

    def first_half(rows4, weight, transposed):
        *pieces, tiles = split_matmul(me, rows4, 0, 0, weight, transposed, size, keep=True)
        return pieces, tiles

    def second_half(rows4, tiles, transposed):
        return split_matmul(me, rows4, 0, 1, tiles, transposed, size, kept=True)


    in_a = exchange(dispatch(selector, far(blocks), 0, peers))
    in_b = exchange(after(dispatch(selector, far(blocks), 1, peers), in_a))
    gates_a, own_a = [], []
    for h in range(2):
        if h == 0:
            pieces, tiles = first_half(in_a, w_enc, False)
        else:
            pieces = second_half(in_a, tiles, False)
        pieces = swap_pieces(pieces, size)
        gate, act = activate(pieces, bias_enc)
        gates_a.append(gate)
        own_a.append(act)
    pieces_a = spread(own_a[0], size) + spread(own_a[1], size)
    enc_b = share(in_b, 0, w_enc, False, True)
    enc_b = swap_pieces(enc_b, size)
    part_a, act_a = decode(me, pieces_a, w_dec, peers, slot_rows, 1, 0, size)
    back_a = exchange(part_a)
    gate_b, own_b = activate(enc_b, bias_enc)
    pieces_b = spread(own_b, size)
    part_b, act_b = decode(me, pieces_b, w_dec, peers, slot_rows, 2, 0, size)
    mixed = residual_rows(selector, back_a, 0, blocks, 0, bias_dec, scale, part_b, 1)
    mixed = far(exchange(mixed))
    resid_b = residual_rows(selector, mixed, 0, blocks, 1, bias_dec, scale, None, 0)
    last = exchange(resid_b)
    back = share(mixed, 1, w_dec, True)
    back = swap_pieces(back, size)
    dec_sum = outer_sum(me, act_a, None, [mixed], 1, None, size, False)
    back[0] = after(back[0], dec_sum)
    gp_a = grad_pre(back, gates_a, 0)
    pre_a = spread(gp_a, size)
    backs = []
    for h in range(2):
        if h == 0:
            pieces, tiles = first_half(last, w_dec, True)
        else:
            pieces = second_half(last, tiles, True)
        backs.append(swap_pieces(pieces, size))
    enc_sum, in_b = outer_sum(me, in_a, 0, pre_a, None, None, size, True, in_b)
    half = gate_b.shape[0] // 2
    pre_b = []
    for h in range(2):
        pieces = backs[h]
        if h == 0:
            pieces[0] = after(pieces[0], enc_sum)
        gp_b = grad_pre(pieces, [gate_b], h * half)
        pre_b += spread(gp_b, size)
    grad_dec = outer_sum(me, act_b, None, [last], 0, dec_sum, size, False)
    grad_enc = encoder_sum(me, in_b, pre_b, enc_sum, size)
    return grad_enc, grad_dec


def solution(mesh):
    in_specs = (
        P("dict", "dp"),
        P("dict", None),
        P("dp", "dict"),
        P("dict", "dp"),
        P("dict"),
        P("dp"),
    )
    out_specs = (P("dp", "dict"), P("dict", "dp"))
    return jax.shard_map(
        on_device, mesh=mesh, in_specs=in_specs, out_specs=out_specs, check_vma=False
    )
```

```python
import jax
import jax.numpy as jnp
from jax import lax
from jax.experimental import pallas as pl
from jax.experimental.pallas import tpu as pltpu
from jax.sharding import PartitionSpec as P


CHUNKS = 2
F32 = jnp.float32
BF16 = jnp.bfloat16
VMEM = pltpu.VMEM


def dot(a, b, dims=((1,), (0,))):
    return lax.dot_general(a, b, (dims, ((), ())), preferred_element_type=F32)


def after(value, *others):
    return lax.optimization_barrier((value,) + others)[0]


def ring(size, shift):
    return [(i, (i + shift) % size) for i in range(size)]


def params(mib=12):
    return pltpu.CompilerParams(vmem_limit_bytes=mib * 1024 * 1024)


def near(value):
    return pltpu.with_memory_space_constraint(value, VMEM)


def far(value):
    return pltpu.with_memory_space_constraint(value, pltpu.HBM)


def whole():
    return pl.BlockSpec(memory_space=VMEM)


def split_matmul(me, rows4, lane, half, weight, transposed, size, tile=512, keep=False, kept=False, away=False, wire=BF16):
    peers, _, slot_rows, inner = rows4.shape
    halves = 2 if half is None else 1
    my_peers = peers * halves // 2
    first = 0 if half is None else half * my_peers
    count = my_peers * slot_rows
    quarter = count // (size * halves)
    if kept:
        tiles = weight.shape
        outer = tiles[0] * (tiles[1] if transposed else tiles[2])
    else:
        outer = weight.shape[0] if transposed else weight.shape[1]
        tiles = (outer // tile, tile, inner) if transposed else (outer // tile, inner, tile)
    tile = outer // tiles[0]

    def body(me_ref, x_any, w_any, *rest):
        own_ref, sends, rest = rest[0], rest[1:size], rest[size:]
        if keep:
            w_ref, rest = rest[0], rest[1:]
        if kept:
            w_ref = w_any
        acc, x_ref, x_sem = rest[:3]
        if not (keep or kept):
            w_ref = rest[3]
        w_sem = rest[-1]

        def fetch(n):
            cols = pl.ds(n * tile, tile)
            source = w_any.at[cols, :] if transposed else w_any.at[:, cols]
            return pltpu.make_async_copy(source, w_ref.at[n], w_sem.at[n])

        x_copy = pltpu.make_async_copy(x_any.at[pl.ds(first, my_peers), lane], x_ref, x_sem)
        x_copy.start()
        if not kept:
            for n in range(tiles[0]):
                fetch(n).start()
        x_copy.wait()

        for n in range(tiles[0]):
            if not kept:
                fetch(n).wait()
            rows = x_ref[...].reshape(count, inner)
            dims = ((1,), (1,)) if transposed else ((1,), (0,))
            acc[:, n * tile : (n + 1) * tile] = dot(rows, w_ref[n], dims)

        mine = me_ref[0]
        for h in range(halves):
            to = pl.ds(h * quarter, quarter)

            def piece(index):
                start = pl.multiple_of((index + h * size) * quarter, quarter)
                return acc[pl.ds(start, quarter), :]

            own_ref[to, :] = piece(mine)
            for shift in range(1, size):
                sends[shift - 1][to, :] = piece(lax.rem(mine + shift, size)).astype(wire)

    return pl.pallas_call(
        body,
        in_specs=[
            pl.BlockSpec(memory_space=pltpu.SMEM),
            pl.BlockSpec(memory_space=pl.ANY),
            whole() if kept else pl.BlockSpec(memory_space=pltpu.HBM),
        ],
        out_specs=[pl.BlockSpec((halves * quarter, outer), lambda: (0, 0)) if away else whole()]
        + [whole()] * (size - 1 + (1 if keep else 0)),
        out_shape=[(pltpu.HBM if away else jax.ShapeDtypeStruct)((halves * quarter, outer), F32)]
        + [jax.ShapeDtypeStruct((halves * quarter, outer), wire)] * (size - 1)
        + ([VMEM(tiles, BF16)] if keep else []),
        scratch_shapes=[
            pltpu.VMEM((count, outer), F32),
            pltpu.VMEM((my_peers, slot_rows, inner), BF16),
            pltpu.SemaphoreType.DMA,
        ]
        + ([] if keep or kept else [pltpu.VMEM(tiles, BF16)])
        + ([] if kept else [pltpu.SemaphoreType.DMA((tiles[0],))]),
        compiler_params=params(20),
        name="split_matmul",
    )(me, rows4, near(weight) if kept else weight)


def assemble(me, parts, out_ref, size):
    quarter = out_ref.shape[0] // (2 * size)
    for i, part in enumerate(parts):
        owner = lax.rem(me + size - i % size, size)
        for j in range(part.shape[0] // quarter):
            index = owner + (i // size + j) * size
            to = pl.ds(pl.multiple_of(index * quarter, quarter), quarter)
            out_ref[to, :] = part[pl.ds(j * quarter, quarter), :]


def decode(me, pieces, w_dec, peers, slot_rows, lanes, lane, size):
    count = peers * slot_rows
    inner, outer = w_dec.shape
    tile = 1024

    def body(me_ref, *refs):
        parts, w_ref, out_ref, act_ref = refs[:-3], refs[-3], refs[-2], refs[-1]
        step = pl.program_id(0)

        @pl.when(step == 0)
        def _():
            assemble(me_ref[0], parts, act_ref, size)

        part = dot(act_ref[...], w_ref[...]).astype(BF16)
        out_ref[...] = part.reshape(peers, 1, slot_rows, tile)

    return pl.pallas_call(
        body,
        grid=(outer // tile,),
        in_specs=[pl.BlockSpec(memory_space=pltpu.SMEM)]
        + [whole()] * len(pieces)
        + [pl.BlockSpec((inner, tile), lambda n: (0, n))],
        out_specs=[
            pl.BlockSpec((peers, 1, slot_rows, tile), lambda n: (0, lane, 0, n)),
            pl.BlockSpec((count, inner), lambda n: (0, 0)),
        ],
        out_shape=[
            pltpu.HBM((peers, lanes, slot_rows, outer), BF16),
            pltpu.HBM((count, inner), BF16),
        ],
        compiler_params=params(24),
        name="decode",
    )(me, *pieces, w_dec)


def residual_rows(selector, returned, lane, blocks, chunk, bias_dec, scale, target, target_lane):
    peers, _, slot_rows, cols = returned.shape
    count = peers * slot_rows
    home = selector.shape[1]
    block_count, rows_block, _ = blocks.shape
    tile = 1024

    def body(sel_ref, got_ref, x_ref, b_ref, *rest):
        out_ref = rest[-1]
        sel = sel_ref[...]
        rebuilt = dot(sel, got_ref[...].reshape(count, tile), ((0,), (0,))) + b_ref[...]
        rows = x_ref[...].reshape(home, tile)
        residual = ((rebuilt - rows.astype(F32)) * scale).astype(BF16)
        out_ref[...] = dot(sel, residual).astype(BF16).reshape(peers, 1, slot_rows, tile)

    in_specs = [
        whole(),
        pl.BlockSpec((peers, 1, slot_rows, tile), lambda n: (0, lane, 0, n)),
        pl.BlockSpec((block_count, rows_block // CHUNKS, tile), lambda n: (0, chunk, n)),
        pl.BlockSpec((1, tile), lambda n: (0, n)),
    ]
    operands = [selector, returned, blocks, bias_dec]
    aliases = {}
    lanes = 1
    if target is not None:
        in_specs.append(pl.BlockSpec(memory_space=pltpu.HBM))
        operands.append(target)
        aliases = {4: 0}
        lanes = target.shape[1]
    return pl.pallas_call(
        body,
        grid=(cols // tile,),
        in_specs=in_specs,
        out_specs=pl.BlockSpec((peers, 1, slot_rows, tile), lambda n: (0, target_lane, 0, n)),
        out_shape=pltpu.HBM((peers, lanes, slot_rows, cols), BF16),
        input_output_aliases=aliases,
        compiler_params=params(24),
        name="residual_rows",
    )(*operands)


def outer_sum(me, left, left_lane, right, right_lane, base, size, inside, carry=None):
    pieces = right_lane is None
    if left_lane is None:
        count, wide = left.shape
    else:
        count, wide = left.shape[0] * left.shape[2], left.shape[3]
    out_cols = right[0].shape[-1]
    last = base is not None
    tile = 512 if last and inside else 1024

    def body(me_ref, left_ref, *refs):
        right_refs = refs[: len(right)]
        out_ref = refs[len(right) + (1 if last or carry is not None else 0)]
        step = pl.program_id(0)
        if carry is not None:
            copy = pltpu.make_async_copy(refs[len(right)], refs[len(right) + 2], refs[-1])
            copy.start()
        here = pl.ds(pl.multiple_of(step * tile, tile), tile)
        lhs = left_ref[...].reshape(count, wide)
        if pieces:
            rows_ref = refs[-1 if carry is None else -2]

            @pl.when(step == 0)
            def _():
                assemble(me_ref[0], right_refs, rows_ref, size)

            rhs = rows_ref[:, here]
        else:
            rhs = right_refs[0][...].reshape(count, tile)
        total = dot(lhs, rhs, ((0,), (0,)))
        if last:
            base_ref = refs[len(right)]
            out_ref[...] = (total + base_ref[:, here]).astype(BF16)
        elif inside:
            out_ref[:, here] = total
        else:
            out_ref[...] = total
        if carry is not None:
            copy.wait()

    column_block = pl.BlockSpec((wide, tile), lambda n: (0, n))
    in_specs = [pl.BlockSpec(memory_space=pltpu.SMEM)]
    operands = [me, left]
    if left_lane is None:
        in_specs.append(pl.BlockSpec((count, wide), lambda n: (0, 0)))
    else:
        operands[1] = near(left)
        in_specs.append(whole())
    if pieces:
        in_specs += [whole()] * len(right)
    else:
        peers, _, slot_rows, _ = right[0].shape
        in_specs.append(
            pl.BlockSpec((peers, 1, slot_rows, tile), lambda n: (0, right_lane, 0, n))
        )
    operands += right
    if last:
        operands.append(near(base))
        in_specs.append(whole())
    if last:
        out_shape = jax.ShapeDtypeStruct((wide, out_cols), BF16)
    else:
        out_shape = (VMEM if inside else pltpu.HBM)((wide, out_cols), F32)
    out_specs = whole() if inside and not last else column_block
    scratch = [pltpu.VMEM((count, out_cols), BF16)] if pieces else []
    if carry is not None:
        assert out_cols == tile
        operands.append(carry)
        in_specs.append(pl.BlockSpec(memory_space=pl.ANY))
        out_shape = [out_shape, VMEM(carry.shape, carry.dtype)]
        out_specs = [out_specs, whole()]
        scratch.append(pltpu.SemaphoreType.DMA)
    return pl.pallas_call(
        body,
        grid=(out_cols // tile,),
        in_specs=in_specs,
        out_specs=out_specs,
        out_shape=out_shape,
        scratch_shapes=scratch,
        compiler_params=params(22 if last else 30),
        name="outer_sum",
    )(*operands)


def encoder_sum(me, left, pieces, base, size):
    peers, _, slot_rows, wide = left.shape
    count = peers * slot_rows
    cols = pieces[0].shape[1]
    tile = 512

    def body(me_ref, left_ref, *refs):
        rows_ref = refs[-1]
        step = pl.program_id(0)
        here = pl.ds(pl.multiple_of(step * tile, tile), tile)

        @pl.when(step == 0)
        def _():
            assemble(me_ref[0], refs[: len(pieces)], rows_ref, size)

        lhs = left_ref[:, 0, :, here].reshape(count, tile)
        total = dot(lhs, rows_ref[...], ((0,), (0,)))
        refs[-2][...] = (total + refs[-3][here, :]).astype(BF16)

    return pl.pallas_call(
        body,
        grid=(wide // tile,),
        in_specs=[
            pl.BlockSpec(memory_space=pltpu.SMEM),
            whole(),
        ]
        + [whole()] * (len(pieces) + 1),
        out_specs=pl.BlockSpec((tile, cols), lambda n: (n, 0)),
        out_shape=jax.ShapeDtypeStruct((wide, cols), BF16),
        scratch_shapes=[pltpu.VMEM((count, cols), BF16)],
        compiler_params=params(20),
        name="encoder_sum",
    )(me, near(left), *pieces, near(base))


def dispatch(selector, blocks, chunk, peers):
    count, home = selector.shape
    block_count, rows_block, cols = blocks.shape
    sub = rows_block // CHUNKS
    tile = 1024

    def body(sel_ref, x_ref, out_ref):
        out = dot(sel_ref[...], x_ref[...].reshape(home, tile)).astype(BF16)
        out_ref[...] = out.reshape(out_ref.shape)

    return pl.pallas_call(
        body,
        grid=(cols // tile,),
        in_specs=[
            whole(),
            pl.BlockSpec((block_count, sub, tile), lambda n: (0, chunk, n)),
        ],
        out_specs=pl.BlockSpec((peers, 1, count // peers, tile), lambda n: (0, 0, 0, n)),
        out_shape=pltpu.HBM((peers, 1, count // peers, cols), BF16),
        compiler_params=params(),
        name="dispatch",
    )(selector, blocks)


def exchange(rows4):
    peers, lanes, slot_rows, cols = rows4.shape
    flat = rows4.reshape(peers, lanes * slot_rows, cols)
    got = lax.all_to_all(flat, "dict", split_axis=0, concat_axis=0, tiled=True)
    return got.reshape(rows4.shape)


def swap_pieces(pieces, size):
    out = [pieces[0]]
    for shift in range(1, size):
        out.append(lax.ppermute(pieces[shift], "dp", ring(size, shift)))
    return out


def total_of(refs):
    total = refs[0][...]
    for ref in refs[1:]:
        total = total + ref[...].astype(F32)
    return total


def activate(pieces, bias_enc):
    def body(*refs):
        gate_ref, act_ref = refs[-2:]
        gate = jnp.maximum(total_of(refs[:-3]) + refs[-3][...], 0.0)
        gate_ref[...] = gate
        act_ref[...] = (gate * gate).astype(BF16)

    shape = pieces[0].shape
    return pl.pallas_call(
        body,
        in_specs=[whole()] * (len(pieces) + 1),
        out_specs=[pl.BlockSpec(shape, lambda: (0, 0)), whole()],
        out_shape=[pltpu.HBM(shape, F32), jax.ShapeDtypeStruct(shape, BF16)],
        compiler_params=params(),
        name="activate",
    )(*pieces, bias_enc)


def grad_pre(pieces, gates, start):
    rows = pieces[0].shape[0]
    size = len(pieces)

    def body(*refs):
        total = total_of(refs[:size])
        done = 0
        for ref in refs[size:-1]:
            count = min(rows - done, ref.shape[0])
            part = total[done : done + count] * 2.0 * ref[pl.ds(start, count), :]
            refs[-1][pl.ds(done, count), :] = part.astype(BF16)
            done += count

    return pl.pallas_call(
        body,
        in_specs=[whole()] * (size + len(gates)),
        out_specs=whole(),
        out_shape=jax.ShapeDtypeStruct(pieces[0].shape, BF16),
        compiler_params=params(),
        name="grad_pre",
    )(*pieces, *gates)


def spread(own, size):
    out = [own]
    for shift in range(1, size):
        out.append(lax.ppermute(own, "dp", ring(size, shift)))
    return out


def on_device(acts, lists, w_enc, w_dec, b_enc, b_dec):
    peers = lax.axis_size("dict")
    size = lax.axis_size("dp")
    me = lax.axis_index("dp").reshape(1).astype(jnp.int32)
    block_count, active_count = lists.shape
    rows_block = acts.shape[0] // block_count
    cols = acts.shape[1]
    capacity = max(2, (2 * block_count * active_count + peers - 1) // peers)
    slot_total = peers * capacity
    sub = rows_block // CHUNKS
    slot_rows = capacity * sub

    flat_ids = lists.reshape(-1)
    onehot = (flat_ids[:, None] == jnp.arange(peers, dtype=jnp.int32)[None, :]).astype(jnp.int32)
    rank_index = jnp.sum((jnp.cumsum(onehot, axis=0) - 1) * onehot, axis=1)
    slot_index = flat_ids * capacity + rank_index
    item_block = jnp.arange(block_count * active_count, dtype=jnp.int32) // active_count
    hit = jnp.arange(slot_total, dtype=jnp.int32)[:, None] == slot_index[None, :]
    slot_block = jnp.sum(jnp.where(hit, item_block[None, :] + 1, 0), axis=1) - 1
    slot_row = slot_block[:, None] * sub + jnp.arange(sub, dtype=jnp.int32)[None, :]
    slot_row = jnp.where(slot_block[:, None] >= 0, slot_row, -1).reshape(-1)
    selector = (
        slot_row[:, None] == jnp.arange(block_count * sub, dtype=jnp.int32)[None, :]
    ).astype(BF16)

    blocks = acts.reshape(block_count, rows_block, cols)
    bias_enc = b_enc.astype(F32).reshape(1, -1)
    bias_dec = b_dec.astype(F32).reshape(1, cols)
    scale = 1.0 / rows_block
    w_enc = far(w_enc)
    w_dec = far(w_dec)

    def share(rows4, lane, weight, transposed, away=False):
        wire = BF16 if transposed else F32
        return split_matmul(
            me, rows4, lane, None, weight, transposed, size, away=away, wire=wire
        )

    def first_half(rows4, weight, transposed):
        wire = BF16 if transposed else F32
        *pieces, tiles = split_matmul(
            me, rows4, 0, 0, weight, transposed, size, keep=True, wire=wire
        )
        return pieces, tiles

    def second_half(rows4, tiles, transposed):
        wire = BF16 if transposed else F32
        return split_matmul(me, rows4, 0, 1, tiles, transposed, size, kept=True, wire=wire)


    in_a = exchange(dispatch(selector, far(blocks), 0, peers))
    in_b = exchange(after(dispatch(selector, far(blocks), 1, peers), in_a))
    gates_a, own_a = [], []
    for h in range(2):
        if h == 0:
            pieces, tiles = first_half(in_a, w_enc, False)
        else:
            pieces = second_half(in_a, tiles, False)
        pieces = swap_pieces(pieces, size)
        gate, act = activate(pieces, bias_enc)
        gates_a.append(gate)
        own_a.append(act)
    pieces_a = spread(own_a[0], size) + spread(own_a[1], size)
    enc_b = share(in_b, 0, w_enc, False, True)
    enc_b = swap_pieces(enc_b, size)
    part_a, act_a = decode(me, pieces_a, w_dec, peers, slot_rows, 1, 0, size)
    back_a = exchange(part_a)
    gate_b, own_b = activate(enc_b, bias_enc)
    pieces_b = spread(own_b, size)
    part_b, act_b = decode(me, pieces_b, w_dec, peers, slot_rows, 2, 0, size)
    mixed = residual_rows(selector, back_a, 0, blocks, 0, bias_dec, scale, part_b, 1)
    mixed = far(exchange(mixed))
    resid_b = residual_rows(selector, mixed, 0, blocks, 1, bias_dec, scale, None, 0)
    last = exchange(resid_b)
    back = share(mixed, 1, w_dec, True)
    back = swap_pieces(back, size)
    dec_sum = outer_sum(me, act_a, None, [mixed], 1, None, size, False)
    back[0] = after(back[0], dec_sum)
    gp_a = grad_pre(back, gates_a, 0)
    pre_a = spread(gp_a, size)
    backs = []
    for h in range(2):
        if h == 0:
            pieces, tiles = first_half(last, w_dec, True)
        else:
            pieces = second_half(last, tiles, True)
        backs.append(swap_pieces(pieces, size))
    enc_sum, in_b = outer_sum(me, in_a, 0, pre_a, None, None, size, True, in_b)
    half = gate_b.shape[0] // 2
    pre_b = []
    for h in range(2):
        pieces = backs[h]
        if h == 0:
            pieces[0] = after(pieces[0], enc_sum)
        gp_b = grad_pre(pieces, [gate_b], h * half)
        pre_b += spread(gp_b, size)
    grad_dec = outer_sum(me, act_b, None, [last], 0, dec_sum, size, False)
    grad_enc = encoder_sum(me, in_b, pre_b, enc_sum, size)
    return grad_enc, grad_dec


def solution(mesh):
    in_specs = (
        P("dict", "dp"),
        P("dict", None),
        P("dp", "dict"),
        P("dict", "dp"),
        P("dict"),
        P("dp"),
    )
    out_specs = (P("dp", "dict"), P("dict", "dp"))
    return jax.shard_map(
        on_device, mesh=mesh, in_specs=in_specs, out_specs=out_specs, check_vma=False
    )
```
